32 devices in a mesh: dp: 4 (over z), context: 8 (over y, x, core).
Axes of the slice: x: 2, y: 2, z: 4, core: 2. Of those that a mesh axis runs over, the one named last changes fastest.
Arguments:
- hidden_in: bfloat16 [4, 1024, 640], P('dp', 'context'), may hold values from -6 to 6
- block_order: int32 [16], replicated, may hold values from 0 to 15, as said below
- norm_scales: bfloat16 [3072], P(('dp', 'context')), may hold values from -0.5 to 1
- w_query: bfloat16 [640, 1024], P(None, ('dp', 'context')), may hold values from -1 to 1
- w_key: bfloat16 [640, 256], P(None, ('dp', 'context')), may hold values from -1 to 1
- w_value: bfloat16 [640, 256], P(None, ('dp', 'context')), may hold values from -0.25 to 0.25
- w_out: bfloat16 [1024, 640], P(('dp', 'context')), may hold values from -0.1875 to 0.1875
- w_gate: bfloat16 [640, 2048], P(None, ('dp', 'context')), may hold values from -0.25 to 0.25
- w_up: bfloat16 [640, 2048], P(None, ('dp', 'context')), may hold values from -0.25 to 0.25
- w_down: bfloat16 [2048, 640], P(('dp', 'context')), may hold values from -0.125 to 0.125
- cotangent: bfloat16 [4, 1024, 640], P('dp', 'context'), may hold values from -6 to 6
Outputs:
- hidden_out: bfloat16 [4, 1024, 640], P('dp', 'context')
- grad_hidden: float32 [4, 1024, 640], P('dp', 'context')
- grad_scales: float32 [3072], P(('dp', 'context'))
- grad_query: float32 [640, 1024], P(None, ('dp', 'context'))
- grad_key: float32 [640, 256], P(None, ('dp', 'context'))
- grad_value: float32 [640, 256], P(None, ('dp', 'context'))
- grad_out_proj: float32 [1024, 640], P(('dp', 'context'))
- grad_gate: float32 [640, 2048], P(None, ('dp', 'context'))
- grad_up: float32 [640, 2048], P(None, ('dp', 'context'))
- grad_down: float32 [2048, 640], P(('dp', 'context'))
The draws below stay inside these ranges and needn't reach their ends.
Inputs may be any that keep to these rules, and one draw needn't show every extreme that they name: `block_order`: for each c below 8, entries 2c and 2c+1 are a block p and its mirror 16 - 1 - p; every block stands in exactly one slot.
All inputs are finite; a program needn't handle non-finite values.
Results may differ from the reference program's by a relative error of at most 0.02.
Values may be sent and summed in bfloat16 or wider, within the bound.
No kernel may reach another device: no remote copies, remote signals or barrier semaphores. Data moves between devices by JAX's collectives and lax.ppermute only.
A program may use at most 128 MiB of HBM per device.

```python
import math
import jax
import jax.numpy as jnp
from jax import lax

D = 640
HQ = 4
HD = 256
FF = 2048
BLK = 64
NBLK = 16
LEN = 1024
SEQS = 4


def draw_block_order(key, part):
    halfway = NBLK // 2
    chosen = jax.random.permutation(key, halfway).astype(jnp.int32)
    mirrored = (NBLK - 1 - chosen).astype(jnp.int32)
    return jnp.stack([chosen, mirrored], axis=1).reshape(NBLK).astype(jnp.int32)


def draw_hidden_in(key, part):
    result = jnp.clip(jax.random.normal(jax.random.fold_in(key, 301), (SEQS, LEN, D), jnp.float32), -6.0, 6.0)
    return result.astype(jnp.bfloat16)


def draw_norm_scales(key, part):
    result = jax.random.uniform(jax.random.fold_in(key, 201), (4 * D + 2 * HD,), jnp.float32, -0.5, 1.0)
    return result.astype(jnp.bfloat16)


def projection_pair(key):
    spread = 1.0 / math.sqrt(D)
    query_part = jnp.clip(jax.random.normal(jax.random.fold_in(key, 102), (D, HQ * HD), jnp.float32), -4.0, 4.0) * spread
    key_part = jnp.clip(jax.random.normal(jax.random.fold_in(key, 103), (D, HD), jnp.float32), -4.0, 4.0) * spread
    return (query_part, key_part)


def draw_w_query(key, part):
    return projection_pair(key)[0].astype(jnp.bfloat16)


def draw_w_key(key, part):
    return projection_pair(key)[1].astype(jnp.bfloat16)


def levels(stream_key, dims, cuts, low, largest):
    level = 1.0
    for axis_at, shards_of in cuts:
        heights = jax.random.uniform(jax.random.fold_in(jax.random.fold_in(stream_key, 6), axis_at), (shards_of,), jnp.float32, low / len(cuts), largest / len(cuts))
        level = level * jnp.repeat(jnp.exp(heights), dims[axis_at] // shards_of).reshape((-1,) + (1,) * (len(dims) - 1 - axis_at))
    return level


def noise(key, extent, scale, most, cuts=(), kind=jnp.bfloat16):
    gain = levels(key, extent, cuts, -0.22, 0.18) if cuts else 1.0
    array = jax.random.normal(key, extent, jnp.float32) * scale * gain
    return jnp.minimum(jnp.maximum(array, -most), most).astype(kind)


def setup_inputs(seed: int = 0) -> dict:
    arg_keys = jax.random.split(jax.random.key(seed), 12)
    return {
        "hidden_in": draw_hidden_in(jax.random.fold_in(arg_keys[11], 71), 0),
        "block_order": draw_block_order(jax.random.fold_in(arg_keys[11], 71), 0),
        "norm_scales": draw_norm_scales(jax.random.fold_in(arg_keys[11], 71), 0),
        "w_query": draw_w_query(jax.random.fold_in(arg_keys[11], 71), 0),
        "w_key": draw_w_key(jax.random.fold_in(arg_keys[11], 71), 0),
        "w_value": noise(arg_keys[5], (D, HD), D ** -0.5, 0.25, ((1, 32),)),
        "w_out": noise(arg_keys[6], (HQ * HD, D), (HQ * HD) ** -0.5, 0.1875, ((0, 32),)),
        "w_gate": noise(arg_keys[7], (D, FF), D ** -0.5, 0.25, ((1, 32),)),
        "w_up": noise(arg_keys[8], (D, FF), D ** -0.5, 0.25, ((1, 32),)),
        "w_down": noise(arg_keys[9], (FF, D), FF ** -0.5, 0.125, ((0, 32),)),
        "cotangent": noise(arg_keys[10], (SEQS, LEN, D), 1.0, 6.0, ((0, 4), (1, 8))),
    }


NORM_EPS = 1e-06
ROPE_BASE = 1000000.0
GELU_COEF = math.sqrt(2.0 / math.pi)

def dot_lead(left_side, right_side):
    return lax.dot_general(left_side, right_side, (((0,), (0,)), ((), ())), preferred_element_type=jnp.float32)

def dot_last(left_side, right_side):
    return lax.dot_general(left_side, right_side, (((1,), (1,)), ((), ())), preferred_element_type=jnp.float32)

def norm_forward(values, gain_param):
    inverse = lax.rsqrt(lax.optimization_barrier(jnp.mean(values * values, axis=-1, keepdims=True)) + NORM_EPS)
    return (values * inverse * (1.0 + gain_param.astype(jnp.float32)), inverse)

def norm_backward(values, inverse, gain_param, upstream):
    weighted = upstream * (1.0 + gain_param.astype(jnp.float32))
    inner_mean = lax.optimization_barrier(jnp.mean(weighted * values, axis=-1, keepdims=True))
    grad_values = inverse * weighted - values * inverse * inverse * inverse * inner_mean
    last_width = values.shape[-1]
    grad_gain = lax.optimization_barrier(jnp.sum((upstream * values * inverse).reshape(-1, last_width), axis=0))
    return (grad_values, grad_gain)

def rotary_tables(positions, head_dim):
    halfway = head_dim // 2
    indices = jnp.arange(halfway).astype(jnp.float32)
    frequency = jnp.exp(indices * (-2.0 * math.log(ROPE_BASE) / head_dim))
    angles = positions.astype(jnp.float32)[:, None] * frequency[None, :]
    return (jnp.cos(angles), jnp.sin(angles))

def rotate(values, cosine, sine_table):
    halfway = values.shape[-1] // 2
    first_half = values[..., :halfway]
    second_half = values[..., halfway:]
    return jnp.concatenate([first_half * cosine - second_half * sine_table, second_half * cosine + first_half * sine_table], axis=-1)

def rotate_back(grad_terms, cosine, sine_table):
    halfway = grad_terms.shape[-1] // 2
    first_half = grad_terms[..., :halfway]
    second_half = grad_terms[..., halfway:]
    return jnp.concatenate([first_half * cosine + second_half * sine_table, second_half * cosine - first_half * sine_table], axis=-1)

def gelu_pair(gate_raw):
    cubic_arg = gate_raw + 0.044715 * gate_raw * gate_raw * gate_raw
    tangent = jnp.tanh(GELU_COEF * cubic_arg)
    gelu_value = 0.5 * gate_raw * (1.0 + tangent)
    gate_slope = 0.5 * (1.0 + tangent) + 0.5 * gate_raw * (1.0 - tangent * tangent) * GELU_COEF * (1.0 + 3.0 * 0.044715 * gate_raw * gate_raw)
    return (gelu_value, gate_slope)

def scores_of(query_rows, query_pos, key_rows, key_pos, factor):
    scores = dot_last(query_rows, key_rows) * factor
    return jnp.where(key_pos[None, :] <= query_pos[:, None], scores, -jnp.inf)

def attend_rows(query_rows, query_pos, key_rows, value_rows, key_pos, factor):
    scores = scores_of(query_rows, query_pos, key_rows, key_pos, factor)
    highest = lax.optimization_barrier(jnp.max(scores, axis=1, keepdims=True))
    exponent = jnp.exp(scores - highest)
    row_total = lax.optimization_barrier(jnp.sum(exponent, axis=1, keepdims=True))
    probability = (exponent / row_total).astype(jnp.bfloat16)
    mixed_rows = jnp.dot(probability, value_rows, preferred_element_type=jnp.float32)
    return (mixed_rows, (highest + jnp.log(row_total))[:, 0])

def attend_back(query_rows, query_pos, key_rows, value_rows, key_pos, factor, logsum, grad_rows, row_delta):
    scores = scores_of(query_rows, query_pos, key_rows, key_pos, factor)
    probability = jnp.exp(scores - logsum[:, None])
    grad_values = dot_lead(probability.astype(jnp.bfloat16), grad_rows)
    grad_probs = dot_last(grad_rows, value_rows)
    grad_scores = (probability * (grad_probs - row_delta[:, None]) * factor).astype(jnp.bfloat16)
    grad_query_rows = jnp.dot(grad_scores, key_rows, preferred_element_type=jnp.float32)
    grad_key_rows = dot_lead(grad_scores, query_rows)
    return (grad_query_rows, grad_key_rows, grad_values)

def reference(hidden_in, block_order, norm_scales, w_query, w_key, w_value, w_out, w_gate, w_up, w_down, cotangent):
    scale_in = norm_scales[0:D]
    scale_attn = norm_scales[D:2 * D]
    scale_pre = norm_scales[2 * D:3 * D]
    scale_ffw = norm_scales[3 * D:4 * D]
    scale_query = norm_scales[4 * D:4 * D + HD]
    scale_key = norm_scales[4 * D + HD:4 * D + 2 * HD]
    positions = (block_order[:, None] * BLK + jnp.arange(BLK, dtype=jnp.int32)[None, :]).reshape(LEN).astype(jnp.int32)
    cosine, sine_table = rotary_tables(positions, HD)
    factor = 1.0 / math.sqrt(HD)
    block_tok = min(512, LEN)
    blocks = LEN // block_tok
    row_pos = jnp.repeat(positions, HQ).reshape(blocks, block_tok * HQ)

    def one_sequence(carried, inputs):
        tokens, upstream = inputs
        tok_f = tokens.astype(jnp.float32)
        normed_in, inv_in = norm_forward(tok_f, scale_in)
        h_in = normed_in.astype(jnp.bfloat16)
        query_raw = jnp.dot(h_in, w_query, preferred_element_type=jnp.float32).reshape(LEN, HQ, HD)
        key_raw = jnp.dot(h_in, w_key, preferred_element_type=jnp.float32)
        value_raw = jnp.dot(h_in, w_value, preferred_element_type=jnp.float32)
        query_n, inv_q = norm_forward(query_raw, scale_query)
        key_n, inv_k = norm_forward(key_raw, scale_key)
        query_rot = rotate(query_n, cosine[:, None, :], sine_table[:, None, :]).astype(jnp.bfloat16)
        key_rot = rotate(key_n, cosine, sine_table).astype(jnp.bfloat16)
        value_b = value_raw.astype(jnp.bfloat16)
        query_rows = query_rot.reshape(blocks, block_tok * HQ, HD)
        attn_mix, logsum = lax.map(lambda block_args: attend_rows(block_args[0], block_args[1], key_rot, value_b, positions, factor), (query_rows, row_pos))
        mixed_b = attn_mix.astype(jnp.bfloat16).reshape(LEN, HQ * HD)
        attn_raw = jnp.dot(mixed_b, w_out, preferred_element_type=jnp.float32)
        attn_n, inv_a = norm_forward(attn_raw, scale_attn)
        resid = tok_f + attn_n
        normed_pre, inv_pre = norm_forward(resid, scale_pre)
        h_pre = normed_pre.astype(jnp.bfloat16)
        gate_raw = jnp.dot(h_pre, w_gate, preferred_element_type=jnp.float32)
        up_raw = jnp.dot(h_pre, w_up, preferred_element_type=jnp.float32)
        activated, gate_slope = gelu_pair(gate_raw)
        hidden = (activated * up_raw).astype(jnp.bfloat16)
        ffw_raw = jnp.dot(hidden, w_down, preferred_element_type=jnp.float32)
        ffw_n, inv_f = norm_forward(ffw_raw, scale_ffw)
        result = (resid + ffw_n).astype(jnp.bfloat16)
        grad_top = upstream.astype(jnp.float32)
        grad_ffw, gs_ffw = norm_backward(ffw_raw, inv_f, scale_ffw, grad_top)
        grad_ffw_b = grad_ffw.astype(jnp.bfloat16)
        gw_down = dot_lead(hidden, grad_ffw_b)
        grad_mid = dot_last(grad_ffw_b, w_down)
        grad_gate_b = (grad_mid * up_raw * gate_slope).astype(jnp.bfloat16)
        grad_up_b = (grad_mid * activated).astype(jnp.bfloat16)
        gw_gate = dot_lead(h_pre, grad_gate_b)
        gw_up = dot_lead(h_pre, grad_up_b)
        grad_pre = dot_last(grad_gate_b, w_gate) + dot_last(grad_up_b, w_up)
        grad_resid_n, gs_pre = norm_backward(resid, inv_pre, scale_pre, grad_pre)
        grad_resid = grad_top + grad_resid_n
        grad_attn, gs_attn = norm_backward(attn_raw, inv_a, scale_attn, grad_resid)
        grad_attn_b = grad_attn.astype(jnp.bfloat16)
        gw_out = dot_lead(mixed_b, grad_attn_b)
        grad_mixed_b = dot_last(grad_attn_b, w_out).astype(jnp.bfloat16)
        row_delta = lax.optimization_barrier(jnp.sum((grad_mixed_b.astype(jnp.float32) * mixed_b.astype(jnp.float32)).reshape(LEN * HQ, HD), axis=1)).reshape(blocks, block_tok * HQ)
        grad_rows = grad_mixed_b.reshape(blocks, block_tok * HQ, HD)

        def back_block(kv_sums, block_args):
            query_part, pos_part, lse_part, grad_part, delta_part = block_args
            grad_q_part, grad_k_part, grad_v_part = attend_back(query_part, pos_part, key_rot, value_b, positions, factor, lse_part, grad_part, delta_part)
            return ((kv_sums[0] + grad_k_part, kv_sums[1] + grad_v_part), grad_q_part)
        zero_kv = jnp.zeros((LEN, HD), jnp.float32)
        kv_sums, grad_query_rows = lax.scan(back_block, (zero_kv, zero_kv), (query_rows, row_pos, logsum, grad_rows, row_delta))
        grad_key_rot, grad_value_rot = kv_sums
        grad_query_n = rotate_back(grad_query_rows.reshape(LEN, HQ, HD), cosine[:, None, :], sine_table[:, None, :])
        grad_query_v, gs_query = norm_backward(query_raw, inv_q, scale_query, grad_query_n)
        grad_key_n = rotate_back(grad_key_rot, cosine, sine_table)
        grad_key_v, gs_key = norm_backward(key_raw, inv_k, scale_key, grad_key_n)
        grad_query_b = grad_query_v.reshape(LEN, HQ * HD).astype(jnp.bfloat16)
        grad_key_b = grad_key_v.astype(jnp.bfloat16)
        grad_value_b = grad_value_rot.astype(jnp.bfloat16)
        gw_query = dot_lead(h_in, grad_query_b)
        gw_key = dot_lead(h_in, grad_key_b)
        gw_value = dot_lead(h_in, grad_value_b)
        grad_in_n = dot_last(grad_query_b, w_query) + dot_last(grad_key_b, w_key) + dot_last(grad_value_b, w_value)
        grad_tok_n, gs_in = norm_backward(tok_f, inv_in, scale_in, grad_in_n)
        grad_tokens = grad_resid + grad_tok_n
        gs_all = jnp.concatenate([gs_in, gs_attn, gs_pre, gs_ffw, gs_query, gs_key])
        new_terms = (gs_all, gw_query, gw_key, gw_value, gw_out, gw_gate, gw_up, gw_down)
        return (jax.tree.map(jnp.add, carried, new_terms), (result, grad_tokens))
    start_terms = (jnp.zeros((4 * D + 2 * HD,), jnp.float32), jnp.zeros((D, HQ * HD), jnp.float32), jnp.zeros((D, HD), jnp.float32), jnp.zeros((D, HD), jnp.float32), jnp.zeros((HQ * HD, D), jnp.float32), jnp.zeros((D, FF), jnp.float32), jnp.zeros((D, FF), jnp.float32), jnp.zeros((FF, D), jnp.float32))
    grad_sums, seq_outputs = lax.scan(one_sequence, start_terms, (hidden_in, cotangent))
    hidden_out, grad_hidden = seq_outputs
    return (hidden_out, grad_hidden, grad_sums[0], grad_sums[1], grad_sums[2], grad_sums[3], grad_sums[4], grad_sums[5], grad_sums[6], grad_sums[7])
```

```python
import math

import jax
import jax.numpy as jnp
from jax import lax
from jax.sharding import PartitionSpec as P

NORM_EPS = 1e-06
ROPE_BASE = 1000000.0
GELU_COEF = math.sqrt(2.0 / math.pi)


def dot_lead(left_side, right_side):
    return lax.dot_general(
        left_side, right_side, (((0,), (0,)), ((), ())), preferred_element_type=jnp.float32
    )


def dot_last(left_side, right_side):
    return lax.dot_general(
        left_side, right_side, (((1,), (1,)), ((), ())), preferred_element_type=jnp.float32
    )


def norm_forward(values, gain_param):
    inverse = lax.rsqrt(jnp.mean(values * values, axis=-1, keepdims=True) + NORM_EPS)
    return (values * inverse * (1.0 + gain_param.astype(jnp.float32)), inverse)


def norm_backward(values, inverse, gain_param, upstream):
    weighted = upstream * (1.0 + gain_param.astype(jnp.float32))
    inner_mean = jnp.mean(weighted * values, axis=-1, keepdims=True)
    grad_values = inverse * weighted - values * inverse * inverse * inverse * inner_mean
    last_width = values.shape[-1]
    grad_gain = jnp.sum((upstream * values * inverse).reshape(-1, last_width), axis=0)
    return (grad_values, grad_gain)


def rotary_tables(positions, head_dim):
    halfway = head_dim // 2
    indices = jnp.arange(halfway).astype(jnp.float32)
    frequency = jnp.exp(indices * (-2.0 * math.log(ROPE_BASE) / head_dim))
    angles = positions.astype(jnp.float32)[:, None] * frequency[None, :]
    return (jnp.cos(angles), jnp.sin(angles))


def rotate(values, cosine, sine_table):
    halfway = values.shape[-1] // 2
    first_half = values[..., :halfway]
    second_half = values[..., halfway:]
    return jnp.concatenate(
        [
            first_half * cosine - second_half * sine_table,
            second_half * cosine + first_half * sine_table,
        ],
        axis=-1,
    )


def rotate_back(grad_terms, cosine, sine_table):
    halfway = grad_terms.shape[-1] // 2
    first_half = grad_terms[..., :halfway]
    second_half = grad_terms[..., halfway:]
    return jnp.concatenate(
        [
            first_half * cosine + second_half * sine_table,
            second_half * cosine - first_half * sine_table,
        ],
        axis=-1,
    )


def gelu_pair(gate_raw):
    cubic_arg = gate_raw + 0.044715 * gate_raw * gate_raw * gate_raw
    tangent = jnp.tanh(GELU_COEF * cubic_arg)
    gelu_value = 0.5 * gate_raw * (1.0 + tangent)
    gate_slope = 0.5 * (1.0 + tangent) + 0.5 * gate_raw * (1.0 - tangent * tangent) * GELU_COEF * (
        1.0 + 3.0 * 0.044715 * gate_raw * gate_raw
    )
    return (gelu_value, gate_slope)


def log_bits(size):
    return [1 << b for b in range(size.bit_length() - 1)]


def swap(array, axis_name, size, bit):
    return lax.ppermute(array, axis_name, [(i, i ^ bit) for i in range(size)])


def xor_order(bits):
    order = [0]
    for bit in bits:
        order = order + [j ^ bit for j in order]
    return order


def gather_xor(rows, axis_name, size, bits):
    for bit in bits:
        rows = jnp.concatenate([rows, swap(rows, axis_name, size, bit)], axis=0)
    return rows


def scatter_xor(rows, axis_name, size, bits):
    for bit in reversed(bits):
        half = rows.shape[0] // 2
        received = swap(rows[half:].astype(jnp.bfloat16), axis_name, size, bit)
        rows = rows[:half].astype(jnp.float32) + received.astype(jnp.float32)
    return rows


def color_bits(size):
    bits = log_bits(size)
    return (bits[1:], bits[:0:-1])


def gather_tokens(rows, size):
    half = rows.shape[0] // 2
    first, second = color_bits(size)
    both = jnp.concatenate(
        [
            gather_xor(rows[:half], "context", size, first),
            gather_xor(rows[half:], "context", size, second),
        ],
        axis=0,
    )
    return gather_xor(both, "context", size, [1])


def scatter_tokens(rows, size):
    first, second = color_bits(size)
    both = scatter_xor(rows, "context", size, [1])
    half = both.shape[0] // 2
    return jnp.concatenate(
        [
            scatter_xor(both[:half], "context", size, first),
            scatter_xor(both[half:], "context", size, second),
        ],
        axis=0,
    )


def token_slots(size):
    first, second = color_bits(size)
    base = [(j, 0) for j in xor_order(first)] + [(j, 1) for j in xor_order(second)]
    return base + [(j ^ 1, part) for j, part in base]


def gather_true(rows, dp_size, ctx_size, dp_index, ctx_index):
    for name, size, index in (("context", ctx_size, ctx_index), ("dp", dp_size, dp_index)):
        for bit in log_bits(size):
            other = swap(rows, name, size, bit)
            rows = jnp.where(
                (index & bit) != 0,
                jnp.concatenate([other, rows], axis=0),
                jnp.concatenate([rows, other], axis=0),
            )
    return rows


def scatter_true(pieces, dp_size, ctx_size, dp_index, ctx_index, order, wire):
    dp_bits = log_bits(dp_size)
    ctx_bits = log_bits(ctx_size)
    tags = [("dp", bit) for bit in reversed(dp_bits)] + [("context", bit) for bit in reversed(ctx_bits)]
    sizes = {"dp": dp_size, "context": ctx_size}
    places = {"dp": dp_index, "context": ctx_index}
    pieces = pieces.reshape((2,) * len(tags) + pieces.shape[1:])
    for name, bit in order:
        axis = tags.index((name, bit))
        tags.pop(axis)
        mine = (places[name] & bit) // bit
        kept = lax.dynamic_index_in_dim(pieces, mine, axis, keepdims=False)
        sent = lax.dynamic_index_in_dim(pieces, 1 - mine, axis, keepdims=False)
        received = swap(sent.astype(wire), name, sizes[name], bit)
        pieces = kept.astype(jnp.float32) + received.astype(jnp.float32)
    return pieces, tags


def scatter_weights(pieces, dp_size, ctx_size, dp_index, ctx_index):
    dp_order = [("dp", bit) for bit in log_bits(dp_size)]
    ctx_order = [("context", bit) for bit in log_bits(ctx_size)]
    rest = ctx_order[1:]
    sizes = (dp_size, ctx_size, dp_index, ctx_index)
    half = pieces.shape[1] // 2
    first, _ = scatter_true(
        pieces[:, :half], *sizes, ctx_order[:1] + rest + dp_order, jnp.bfloat16
    )
    second, _ = scatter_true(
        pieces[:, half:], *sizes, ctx_order[:1] + dp_order + rest[::-1], jnp.bfloat16
    )
    return jnp.concatenate([first, second], axis=0)


def make_on_device(dp_size, ctx_size):
    def on_device(
        hidden_in, block_order, norm_scales, w_query, w_key, w_value, w_out, w_gate, w_up, w_down, cotangent
    ):
        parts = dp_size * ctx_size
        dp_index = lax.axis_index("dp")
        ctx_index = lax.axis_index("context")
        places = (dp_size, ctx_size, dp_index, ctx_index)
        seq_count, local_tok, width = hidden_in.shape
        n_q, n_k, n_v, n_o = w_query.shape[1], w_key.shape[1], w_value.shape[1], w_out.shape[0]
        n_f = w_gate.shape[1]
        head_dim = n_k * parts
        heads = n_q * parts // head_dim
        block_len = local_tok // 2
        tokens = hidden_in.reshape(local_tok, width)
        attn_pack = jnp.concatenate([w_query.T, w_key.T, w_value.T, w_out], axis=0)
        attn_all = lax.all_gather(attn_pack, ("dp", "context"), axis=0, tiled=False)
        scales = gather_true(norm_scales, *places)
        seq_hidden = gather_tokens(tokens, ctx_size)
        ffn_pack = jnp.concatenate([w_gate.T, w_up.T, w_down], axis=0)
        ffn_all = gather_xor(ffn_pack, "dp", dp_size, log_bits(dp_size)[::-1]).reshape(
            dp_size, 3, n_f, width
        )
        gate_t = ffn_all[:, 0].reshape(dp_size * n_f, width)
        up_t = ffn_all[:, 1].reshape(dp_size * n_f, width)
        down_w = ffn_all[:, 2].reshape(dp_size * n_f, width)
        query_t = attn_all[:, :n_q].reshape(parts * n_q, width)
        key_value_t = jnp.concatenate(
            [
                attn_all[:, n_q : n_q + n_k].reshape(parts * n_k, width),
                attn_all[:, n_q + n_k : n_q + n_k + n_v].reshape(parts * n_v, width),
            ],
            axis=0,
        )
        out_w = attn_all[:, n_q + n_k + n_v :].reshape(parts * n_o, width)
        scale_in = scales[0:width]
        scale_attn = scales[width : 2 * width]
        scale_pre = scales[2 * width : 3 * width]
        scale_ffw = scales[3 * width : 4 * width]
        scale_query = scales[4 * width : 4 * width + head_dim]
        scale_key = scales[4 * width + head_dim : 4 * width + 2 * head_dim]

        slots = token_slots(ctx_size)
        slot_xor = jnp.array([j for j, _ in slots], jnp.int32)
        slot_part = jnp.array([part for _, part in slots], jnp.int32)
        all_blocks = block_order[(ctx_index ^ slot_xor) * 2 + slot_part]
        key_pos = (
            all_blocks[:, None] * block_len + jnp.arange(block_len, dtype=jnp.int32)[None, :]
        ).reshape(-1)
        own_blocks = lax.dynamic_slice_in_dim(block_order, ctx_index * 2, 2)
        local_pos = (
            own_blocks[:, None] * block_len + jnp.arange(block_len, dtype=jnp.int32)[None, :]
        ).reshape(-1)
        cos_q, sin_q = rotary_tables(local_pos, head_dim)
        cos_k, sin_k = rotary_tables(key_pos, head_dim)
        factor = 1.0 / math.sqrt(head_dim)

        tok_f = tokens.astype(jnp.float32)
        normed_in, inv_in = norm_forward(tok_f, scale_in)
        h_in = normed_in.astype(jnp.bfloat16)
        seq_normed, _ = norm_forward(seq_hidden.astype(jnp.float32), scale_in)
        kv_raw = dot_last(seq_normed.astype(jnp.bfloat16), key_value_t)
        query_raw = dot_last(h_in, query_t).reshape(local_tok, heads, head_dim)
        key_n, _ = norm_forward(kv_raw[:, :head_dim], scale_key)
        keys = rotate(key_n, cos_k, sin_k).astype(jnp.bfloat16)
        values = kv_raw[:, head_dim:].astype(jnp.bfloat16)
        query_n, inv_q = norm_forward(query_raw, scale_query)
        query_rot = rotate(query_n, cos_q[:, None, :], sin_q[:, None, :]).astype(jnp.bfloat16)
        query_rows = query_rot.transpose(1, 0, 2).reshape(heads * local_tok, head_dim)
        row_pos = jnp.tile(local_pos, heads)
        scores = dot_last(query_rows, keys) * factor
        allowed = key_pos[None, :] <= row_pos[:, None]
        scores = jnp.where(allowed, scores, -jnp.inf)
        highest = jnp.max(scores, axis=1, keepdims=True)
        exponent = jnp.exp(scores - highest)
        row_total = jnp.sum(exponent, axis=1, keepdims=True)
        probability = exponent / row_total
        probs_b = probability.astype(jnp.bfloat16)
        mixed_rows = jnp.dot(probs_b, values, preferred_element_type=jnp.float32).astype(jnp.bfloat16)
        mixed_b = (
            mixed_rows.reshape(heads, local_tok, head_dim)
            .transpose(1, 0, 2)
            .reshape(local_tok, heads * head_dim)
        )
        attn_raw = jnp.dot(mixed_b, out_w, preferred_element_type=jnp.float32)
        attn_n, inv_a = norm_forward(attn_raw, scale_attn)
        resid = tok_f + attn_n
        normed_pre, inv_pre = norm_forward(resid, scale_pre)
        h_pre = gather_tokens(normed_pre.astype(jnp.bfloat16), ctx_size)
        gate_raw = dot_last(h_pre, gate_t)
        up_raw = dot_last(h_pre, up_t)
        activated, gate_slope = gelu_pair(gate_raw)
        hidden = (activated * up_raw).astype(jnp.bfloat16)
        ffw_raw = scatter_tokens(
            jnp.dot(hidden, down_w, preferred_element_type=jnp.float32), ctx_size
        )
        ffw_n, inv_f = norm_forward(ffw_raw, scale_ffw)
        result = (resid + ffw_n).astype(jnp.bfloat16)

        grad_top = cotangent.reshape(local_tok, width).astype(jnp.float32)
        grad_ffw, gs_ffw = norm_backward(ffw_raw, inv_f, scale_ffw, grad_top)
        grad_ffw_b = gather_tokens(grad_ffw.astype(jnp.bfloat16), ctx_size)
        grad_mid = dot_last(grad_ffw_b, down_w)
        grad_gate_b = (grad_mid * up_raw * gate_slope).astype(jnp.bfloat16)
        grad_up_b = (grad_mid * activated).astype(jnp.bfloat16)
        grad_pre = scatter_tokens(
            jnp.dot(grad_gate_b, gate_t, preferred_element_type=jnp.float32)
            + jnp.dot(grad_up_b, up_t, preferred_element_type=jnp.float32),
            ctx_size,
        )
        ffn_terms = jnp.stack(
            [
                dot_lead(grad_gate_b, h_pre).reshape(dp_size, n_f, width),
                dot_lead(grad_up_b, h_pre).reshape(dp_size, n_f, width),
                dot_lead(hidden, grad_ffw_b).reshape(dp_size, n_f, width),
            ],
            axis=1,
        ).astype(jnp.bfloat16)
        ffn_grads = scatter_xor(
            ffn_terms.reshape(dp_size * 3 * n_f, width), "dp", dp_size, log_bits(dp_size)[::-1]
        )
        grad_resid_n, gs_pre = norm_backward(resid, inv_pre, scale_pre, grad_pre)
        grad_resid = grad_top + grad_resid_n
        grad_attn, gs_attn = norm_backward(attn_raw, inv_a, scale_attn, grad_resid)
        grad_attn_b = grad_attn.astype(jnp.bfloat16)
        gw_out = dot_lead(mixed_b, grad_attn_b).astype(jnp.bfloat16)
        out_grads = scatter_weights(gw_out.reshape(parts, n_o, width), *places)
        grad_mixed_b = dot_last(grad_attn_b, out_w).astype(jnp.bfloat16)
        grad_rows = (
            grad_mixed_b.reshape(local_tok, heads, head_dim)
            .transpose(1, 0, 2)
            .reshape(heads * local_tok, head_dim)
        )
        row_delta = jnp.sum(
            grad_rows.astype(jnp.float32) * mixed_rows.astype(jnp.float32), axis=1, keepdims=True
        )
        grad_probs = dot_last(grad_rows, values)
        grad_scores = (probability * (grad_probs - row_delta) * factor).astype(jnp.bfloat16)
        grad_q_rows = jnp.dot(grad_scores, keys, preferred_element_type=jnp.float32)
        grad_kv = scatter_tokens(
            jnp.concatenate(
                [dot_lead(grad_scores, query_rows), dot_lead(probs_b, grad_rows)], axis=1
            ).astype(jnp.bfloat16),
            ctx_size,
        )
        grad_query_n = rotate_back(
            grad_q_rows.reshape(heads, local_tok, head_dim).transpose(1, 0, 2),
            cos_q[:, None, :],
            sin_q[:, None, :],
        )
        grad_query_v, gs_query = norm_backward(query_raw, inv_q, scale_query, grad_query_n)
        grad_query_b = grad_query_v.reshape(local_tok, heads * head_dim).astype(jnp.bfloat16)
        gw_query = dot_lead(grad_query_b, h_in).astype(jnp.bfloat16)
        query_grads = scatter_weights(gw_query.reshape(parts, n_q, width), *places)
        key_raw = dot_last(h_in, key_value_t[:head_dim])
        _, inv_k = norm_forward(key_raw, scale_key)
        grad_key_n = rotate_back(grad_kv[:, :head_dim], cos_q, sin_q)
        grad_key_v, gs_key = norm_backward(key_raw, inv_k, scale_key, grad_key_n)
        grad_kv_b = jnp.concatenate(
            [grad_key_v.astype(jnp.bfloat16), grad_kv[:, head_dim:].astype(jnp.bfloat16)], axis=1
        )
        gw_kv = dot_lead(grad_kv_b, h_in).astype(jnp.bfloat16)
        kv_terms = jnp.concatenate(
            [
                gw_kv[:head_dim].reshape(parts, n_k, width),
                gw_kv[head_dim:].reshape(parts, n_v, width),
            ],
            axis=1,
        )
        kv_grads = scatter_weights(kv_terms, *places)
        grad_in_n = jnp.dot(
            grad_query_b, query_t, preferred_element_type=jnp.float32
        ) + jnp.dot(grad_kv_b, key_value_t, preferred_element_type=jnp.float32)
        grad_tok_n, gs_in = norm_backward(tok_f, inv_in, scale_in, grad_in_n)
        grad_tokens = grad_resid + grad_tok_n
        gs_all = jnp.concatenate([gs_in, gs_attn, gs_pre, gs_ffw, gs_query, gs_key])
        gs_order = [("context", bit) for bit in log_bits(ctx_size)] + [
            ("dp", bit) for bit in log_bits(dp_size)
        ]
        gs_own, _ = scatter_true(
            gs_all.reshape(parts, norm_scales.shape[0]), *places, gs_order, jnp.float32
        )
        return (
            result.reshape(seq_count, local_tok, width),
            grad_tokens.reshape(seq_count, local_tok, width),
            gs_own,
            query_grads.T,
            kv_grads[:n_k].T,
            kv_grads[n_k:].T,
            out_grads,
            ffn_grads[:n_f].T,
            ffn_grads[n_f : 2 * n_f].T,
            ffn_grads[2 * n_f :],
        )

    return on_device


def solution(mesh):
    return jax.shard_map(
        make_on_device(mesh.shape["dp"], mesh.shape["context"]),
        mesh=mesh,
        in_specs=(
            P("dp", "context", None),
            P(),
            P(("dp", "context")),
            P(None, ("dp", "context")),
            P(None, ("dp", "context")),
            P(None, ("dp", "context")),
            P(("dp", "context"), None),
            P(None, ("dp", "context")),
            P(None, ("dp", "context")),
            P(("dp", "context"), None),
            P("dp", "context", None),
        ),
        out_specs=(
            P("dp", "context", None),
            P("dp", "context", None),
            P(("dp", "context")),
            P(None, ("dp", "context")),
            P(None, ("dp", "context")),
            P(None, ("dp", "context")),
            P(("dp", "context"), None),
            P(None, ("dp", "context")),
            P(None, ("dp", "context")),
            P(("dp", "context"), None),
        ),
        check_vma=False,
    )
```

```python
import math

import jax
import jax.numpy as jnp
from jax import lax
from jax.sharding import PartitionSpec as P

NORM_EPS = 1e-06
ROPE_BASE = 1000000.0
GELU_COEF = math.sqrt(2.0 / math.pi)


def dot_lead(left_side, right_side):
    return lax.dot_general(
        left_side, right_side, (((0,), (0,)), ((), ())), preferred_element_type=jnp.float32
    )


def dot_last(left_side, right_side):
    return lax.dot_general(
        left_side, right_side, (((1,), (1,)), ((), ())), preferred_element_type=jnp.float32
    )


def norm_forward(values, gain_param):
    inverse = lax.rsqrt(jnp.mean(values * values, axis=-1, keepdims=True) + NORM_EPS)
    return (values * inverse * (1.0 + gain_param.astype(jnp.float32)), inverse)


def norm_backward(values, inverse, gain_param, upstream):
    weighted = upstream * (1.0 + gain_param.astype(jnp.float32))
    inner_mean = jnp.mean(weighted * values, axis=-1, keepdims=True)
    grad_values = inverse * weighted - values * inverse * inverse * inverse * inner_mean
    last_width = values.shape[-1]
    grad_gain = jnp.sum((upstream * values * inverse).reshape(-1, last_width), axis=0)
    return (grad_values, grad_gain)


def rotary_tables(positions, head_dim):
    halfway = head_dim // 2
    indices = jnp.arange(halfway).astype(jnp.float32)
    frequency = jnp.exp(indices * (-2.0 * math.log(ROPE_BASE) / head_dim))
    angles = positions.astype(jnp.float32)[:, None] * frequency[None, :]
    return (jnp.cos(angles), jnp.sin(angles))


def rotate(values, cosine, sine_table):
    halfway = values.shape[-1] // 2
    first_half = values[..., :halfway]
    second_half = values[..., halfway:]
    return jnp.concatenate(
        [
            first_half * cosine - second_half * sine_table,
            second_half * cosine + first_half * sine_table,
        ],
        axis=-1,
    )


def rotate_back(grad_terms, cosine, sine_table):
    halfway = grad_terms.shape[-1] // 2
    first_half = grad_terms[..., :halfway]
    second_half = grad_terms[..., halfway:]
    return jnp.concatenate(
        [
            first_half * cosine + second_half * sine_table,
            second_half * cosine - first_half * sine_table,
        ],
        axis=-1,
    )


def gelu_pair(gate_raw):
    cubic_arg = gate_raw + 0.044715 * gate_raw * gate_raw * gate_raw
    tangent = jnp.tanh(GELU_COEF * cubic_arg)
    gelu_value = 0.5 * gate_raw * (1.0 + tangent)
    gate_slope = 0.5 * (1.0 + tangent) + 0.5 * gate_raw * (1.0 - tangent * tangent) * GELU_COEF * (
        1.0 + 3.0 * 0.044715 * gate_raw * gate_raw
    )
    return (gelu_value, gate_slope)


def log_bits(size):
    return [1 << b for b in range(size.bit_length() - 1)]


def swap(array, axis_name, size, bit):
    return lax.ppermute(array, axis_name, [(i, i ^ bit) for i in range(size)])


def xor_order(bits):
    order = [0]
    for bit in bits:
        order = order + [j ^ bit for j in order]
    return order


def lockstep(sizes, *chains):
    results = [None] * len(chains)
    sends = {}
    for i, chain in enumerate(chains):
        sends[i] = next(chain)
    while sends:
        flat = [swap(array, name, sizes[name], bit) for i in sends for array, name, bit in sends[i]]
        flat = list(lax.optimization_barrier(tuple(flat)))
        following = {}
        for i in sends:
            count = len(sends[i])
            arrived, flat = flat[:count], flat[count:]
            try:
                following[i] = chains[i].send(arrived)
            except StopIteration as stop:
                results[i] = stop.value
        sends = following
    return results


def resume(sends, chain):
    while True:
        arrived = yield sends
        try:
            sends = chain.send(arrived)
        except StopIteration as stop:
            return stop.value


def gather_xor(rows, axis_name, bits):
    for bit in bits:
        (other,) = yield [(rows, axis_name, bit)]
        rows = jnp.concatenate([rows, other], axis=0)
    return rows


def scatter_xor(rows, axis_name, bits):
    for bit in reversed(bits):
        half = rows.shape[0] // 2
        (other,) = yield [(rows[half:].astype(jnp.bfloat16), axis_name, bit)]
        rows = rows[:half].astype(jnp.float32) + other.astype(jnp.float32)
    return rows


def color_bits(size):
    bits = log_bits(size)
    return (bits[1:], bits[:0:-1])


def gather_tokens(rows, size):
    half = rows.shape[0] // 2
    one, two = rows[:half], rows[half:]
    for bit_one, bit_two in zip(*color_bits(size)):
        other_one, other_two = yield [(one, "context", bit_one), (two, "context", bit_two)]
        one = jnp.concatenate([one, other_one], axis=0)
        two = jnp.concatenate([two, other_two], axis=0)
    both = jnp.concatenate([one, two], axis=0)
    (other,) = yield [(both, "context", 1)]
    return jnp.concatenate([both, other], axis=0)


def scatter_tokens(rows, size):
    half = rows.shape[0] // 2
    (other,) = yield [(rows[half:].astype(jnp.bfloat16), "context", 1)]
    both = rows[:half].astype(jnp.float32) + other.astype(jnp.float32)
    half = both.shape[0] // 2
    one, two = both[:half], both[half:]
    first, second = color_bits(size)
    for bit_one, bit_two in zip(reversed(first), reversed(second)):
        half = one.shape[0] // 2
        other_one, other_two = yield [
            (one[half:].astype(jnp.bfloat16), "context", bit_one),
            (two[half:].astype(jnp.bfloat16), "context", bit_two),
        ]
        one = one[:half].astype(jnp.float32) + other_one.astype(jnp.float32)
        two = two[:half].astype(jnp.float32) + other_two.astype(jnp.float32)
    return jnp.concatenate([one, two], axis=0)


def token_slots(size):
    first, second = color_bits(size)
    base = [(j, 0) for j in xor_order(first)] + [(j, 1) for j in xor_order(second)]
    return base + [(j ^ 1, part) for j, part in base]


def piece_tags(sizes):
    return [("dp", bit) for bit in reversed(log_bits(sizes["dp"]))] + [
        ("context", bit) for bit in reversed(log_bits(sizes["context"]))
    ]


def gather_true(rows, sizes, places, order):
    canonical = piece_tags(sizes)
    tags = []
    for name, bit in order:
        (other,) = yield [(rows, name, bit)]
        tags = sorted(tags + [(name, bit)], key=canonical.index)
        axis = tags.index((name, bit))
        rows = jnp.where(
            (places[name] & bit) != 0,
            jnp.stack([other, rows], axis=axis),
            jnp.stack([rows, other], axis=axis),
        )
    return rows.reshape((-1,) + rows.shape[len(tags) :])


def scatter_true(pieces, sizes, places, order, wire):
    tags = piece_tags(sizes)
    pieces = pieces.reshape((2,) * len(tags) + pieces.shape[1:])
    for name, bit in order:
        axis = tags.index((name, bit))
        tags.pop(axis)
        mine = (places[name] & bit) // bit
        kept = lax.dynamic_index_in_dim(pieces, mine, axis, keepdims=False)
        sent = lax.dynamic_index_in_dim(pieces, 1 - mine, axis, keepdims=False)
        (other,) = yield [(sent.astype(wire), name, bit)]
        pieces = kept.astype(jnp.float32) + other.astype(jnp.float32)
    return pieces


def make_on_device(dp_size, ctx_size):
    def on_device(
        hidden_in, block_order, norm_scales, w_query, w_key, w_value, w_out, w_gate, w_up, w_down, cotangent
    ):
        parts = dp_size * ctx_size
        dp_index = lax.axis_index("dp")
        ctx_index = lax.axis_index("context")
        places = {"dp": dp_index, "context": ctx_index}
        sizes = {"dp": dp_size, "context": ctx_size}
        near = [("context", 1)]
        across = [("context", bit) for bit in log_bits(ctx_size)[1:]]
        along = [("dp", bit) for bit in log_bits(dp_size)]
        seq_count, local_tok, width = hidden_in.shape
        n_q, n_k, n_v, n_o = w_query.shape[1], w_key.shape[1], w_value.shape[1], w_out.shape[0]
        n_f = w_gate.shape[1]
        head_dim = n_k * parts
        heads = n_q * parts // head_dim
        block_len = local_tok // 2
        tokens = hidden_in.reshape(local_tok, width)
        key_value_pack = jnp.concatenate([w_key.T, w_value.T], axis=0)
        query_all, key_value_all, out_all, scales, seq_hidden = lockstep(
            sizes,
            gather_true(w_query.T, sizes, places, along[::-1] + across + near),
            gather_true(key_value_pack, sizes, places, across + along[::-1] + near),
            gather_true(w_out, sizes, places, across[::-1] + along[::-1] + near),
            gather_true(norm_scales, sizes, places, along + across + near),
            gather_tokens(tokens, ctx_size),
        )
        scales = scales.reshape(-1)
        ffn_pack = jnp.concatenate([w_gate.T, w_up.T, w_down], axis=0)
        query_t = query_all.reshape(parts * n_q, width)
        query_t, ffn_pack = lax.optimization_barrier((query_t, ffn_pack))
        load_chain = gather_xor(ffn_pack, "dp", log_bits(dp_size)[::-1])
        ((load_sent, _, load_bit),) = next(load_chain)
        load_got = swap(load_sent, "dp", dp_size, load_bit)
        key_value_t = jnp.concatenate(
            [
                key_value_all[:, :n_k].reshape(parts * n_k, width),
                key_value_all[:, n_k:].reshape(parts * n_v, width),
            ],
            axis=0,
        )
        out_w = out_all.reshape(parts * n_o, width)
        scale_in = scales[0:width]
        scale_attn = scales[width : 2 * width]
        scale_pre = scales[2 * width : 3 * width]
        scale_ffw = scales[3 * width : 4 * width]
        scale_query = scales[4 * width : 4 * width + head_dim]
        scale_key = scales[4 * width + head_dim : 4 * width + 2 * head_dim]

        slots = token_slots(ctx_size)
        slot_xor = jnp.array([j for j, _ in slots], jnp.int32)
        slot_part = jnp.array([part for _, part in slots], jnp.int32)
        all_blocks = block_order[(ctx_index ^ slot_xor) * 2 + slot_part]
        key_pos = (
            all_blocks[:, None] * block_len + jnp.arange(block_len, dtype=jnp.int32)[None, :]
        ).reshape(-1)
        own_blocks = lax.dynamic_slice_in_dim(block_order, ctx_index * 2, 2)
        local_pos = (
            own_blocks[:, None] * block_len + jnp.arange(block_len, dtype=jnp.int32)[None, :]
        ).reshape(-1)
        cos_q, sin_q = rotary_tables(local_pos, head_dim)
        cos_k, sin_k = rotary_tables(key_pos, head_dim)
        factor = 1.0 / math.sqrt(head_dim)

        tok_f = tokens.astype(jnp.float32)
        normed_in, inv_in = norm_forward(tok_f, scale_in)
        h_in = normed_in.astype(jnp.bfloat16)
        seq_f = seq_hidden.astype(jnp.float32)
        seq_normed, seq_inv = norm_forward(seq_f, scale_in)
        seq_h = seq_normed.astype(jnp.bfloat16)
        kv_raw = dot_last(seq_h, key_value_t)
        query_raw = dot_last(h_in, query_t).reshape(local_tok, heads, head_dim)
        key_raw = kv_raw[:, :head_dim]
        key_n, inv_k = norm_forward(key_raw, scale_key)
        keys = rotate(key_n, cos_k, sin_k).astype(jnp.bfloat16)
        values = kv_raw[:, head_dim:].astype(jnp.bfloat16)
        query_n, inv_q = norm_forward(query_raw, scale_query)
        query_rot = rotate(query_n, cos_q[:, None, :], sin_q[:, None, :]).astype(jnp.bfloat16)
        query_rows = query_rot.transpose(1, 0, 2).reshape(heads * local_tok, head_dim)
        load_got, query_rows = lax.optimization_barrier((load_got, query_rows))
        (ffn_flat,) = lockstep(sizes, resume(load_chain.send([load_got]), load_chain))
        ffn_all = ffn_flat.reshape(dp_size, 3, n_f, width)
        gate_t = ffn_all[:, 0].reshape(dp_size * n_f, width)
        up_t = ffn_all[:, 1].reshape(dp_size * n_f, width)
        down_w = ffn_all[:, 2].reshape(dp_size * n_f, width)
        row_pos = jnp.tile(local_pos, heads)
        scores = dot_last(query_rows, keys) * factor
        allowed = key_pos[None, :] <= row_pos[:, None]
        scores = jnp.where(allowed, scores, -jnp.inf)
        highest = jnp.max(scores, axis=1, keepdims=True)
        exponent = jnp.exp(scores - highest)
        row_total = jnp.sum(exponent, axis=1, keepdims=True)
        probability = exponent / row_total
        probs_b = probability.astype(jnp.bfloat16)
        mixed_rows = jnp.dot(probs_b, values, preferred_element_type=jnp.float32).astype(jnp.bfloat16)
        mixed_b = (
            mixed_rows.reshape(heads, local_tok, head_dim)
            .transpose(1, 0, 2)
            .reshape(local_tok, heads * head_dim)
        )
        attn_raw = jnp.dot(mixed_b, out_w, preferred_element_type=jnp.float32)
        attn_n, inv_a = norm_forward(attn_raw, scale_attn)
        resid = tok_f + attn_n
        normed_pre, inv_pre = norm_forward(resid, scale_pre)
        (h_pre,) = lockstep(sizes, gather_tokens(normed_pre.astype(jnp.bfloat16), ctx_size))
        gate_raw = dot_last(h_pre, gate_t)
        up_raw = dot_last(h_pre, up_t)
        activated, gate_slope = gelu_pair(gate_raw)
        hidden = (activated * up_raw).astype(jnp.bfloat16)
        ffw_part = jnp.dot(hidden, down_w, preferred_element_type=jnp.float32)
        (ffw_raw,) = lockstep(sizes, scatter_tokens(ffw_part, ctx_size))
        ffw_n, inv_f = norm_forward(ffw_raw, scale_ffw)
        result = (resid + ffw_n).astype(jnp.bfloat16)

        grad_top = cotangent.reshape(local_tok, width).astype(jnp.float32)
        grad_ffw, gs_ffw = norm_backward(ffw_raw, inv_f, scale_ffw, grad_top)
        (grad_ffw_b,) = lockstep(sizes, gather_tokens(grad_ffw.astype(jnp.bfloat16), ctx_size))
        grad_mid = dot_last(grad_ffw_b, down_w)
        grad_gate_b = (grad_mid * up_raw * gate_slope).astype(jnp.bfloat16)
        grad_up_b = (grad_mid * activated).astype(jnp.bfloat16)
        pre_part = jnp.dot(grad_gate_b, gate_t, preferred_element_type=jnp.float32) + jnp.dot(
            grad_up_b, up_t, preferred_element_type=jnp.float32
        )
        (grad_pre,) = lockstep(sizes, scatter_tokens(pre_part, ctx_size))
        ffn_terms = jnp.stack(
            [
                dot_lead(grad_gate_b, h_pre).reshape(dp_size, n_f, width),
                dot_lead(grad_up_b, h_pre).reshape(dp_size, n_f, width),
                dot_lead(hidden, grad_ffw_b).reshape(dp_size, n_f, width),
            ],
            axis=1,
        ).astype(jnp.bfloat16)
        grad_pre, ffn_terms = lax.optimization_barrier((grad_pre, ffn_terms))
        ffn_chain = scatter_xor(
            ffn_terms.reshape(dp_size * 3 * n_f, width), "dp", log_bits(dp_size)[::-1]
        )
        ((ffn_sent, _, ffn_bit),) = next(ffn_chain)
        ffn_got = swap(ffn_sent, "dp", dp_size, ffn_bit)
        grad_resid_n, gs_pre = norm_backward(resid, inv_pre, scale_pre, grad_pre)
        grad_resid = grad_top + grad_resid_n
        grad_attn, gs_attn = norm_backward(attn_raw, inv_a, scale_attn, grad_resid)
        grad_attn_b = grad_attn.astype(jnp.bfloat16)
        gw_out = dot_lead(mixed_b, grad_attn_b).astype(jnp.bfloat16)
        grad_mixed_b = dot_last(grad_attn_b, out_w).astype(jnp.bfloat16)
        grad_rows = (
            grad_mixed_b.reshape(local_tok, heads, head_dim)
            .transpose(1, 0, 2)
            .reshape(heads * local_tok, head_dim)
        )
        row_delta = jnp.sum(
            grad_rows.astype(jnp.float32) * mixed_rows.astype(jnp.float32), axis=1, keepdims=True
        )
        grad_probs = dot_last(grad_rows, values)
        grad_scores = (probability * (grad_probs - row_delta) * factor).astype(jnp.bfloat16)
        ffn_got, grad_scores = lax.optimization_barrier((ffn_got, grad_scores))
        grad_q_rows = jnp.dot(grad_scores, keys, preferred_element_type=jnp.float32)
        grad_key_rot = dot_lead(grad_scores, query_rows)
        grad_value_b = dot_lead(probs_b, grad_rows).astype(jnp.bfloat16)
        grad_key_n = rotate_back(grad_key_rot, cos_k, sin_k)
        grad_key_v, gs_key = norm_backward(key_raw, inv_k, scale_key, grad_key_n)
        grad_kv_b = jnp.concatenate([grad_key_v.astype(jnp.bfloat16), grad_value_b], axis=1)
        gw_kv = dot_lead(grad_kv_b, seq_h).astype(jnp.bfloat16)
        seq_grad = jnp.dot(grad_kv_b, key_value_t, preferred_element_type=jnp.float32)
        gs_seq = jnp.sum(seq_grad * seq_f * seq_inv, axis=0)
        grad_query_n = rotate_back(
            grad_q_rows.reshape(heads, local_tok, head_dim).transpose(1, 0, 2),
            cos_q[:, None, :],
            sin_q[:, None, :],
        )
        grad_query_v, gs_query = norm_backward(query_raw, inv_q, scale_query, grad_query_n)
        grad_query_b = grad_query_v.reshape(local_tok, heads * head_dim).astype(jnp.bfloat16)
        gw_query = dot_lead(grad_query_b, h_in).astype(jnp.bfloat16)
        kv_terms = jnp.concatenate(
            [
                gw_kv[:head_dim].reshape(parts, n_k, width),
                gw_kv[head_dim:].reshape(parts, n_v, width),
            ],
            axis=1,
        )
        own_grad = jnp.dot(grad_query_b, query_t, preferred_element_type=jnp.float32)
        gs_own_in = jnp.sum(own_grad * tok_f * inv_in, axis=0)
        gs_all = jnp.concatenate(
            [gs_seq + gs_own_in, gs_attn, gs_pre, gs_ffw, gs_query, gs_key]
        ).reshape(parts, norm_scales.shape[0])
        seq_part, query_grads, kv_grads, out_grads, gs_own, ffn_grads = lockstep(
            sizes,
            scatter_tokens(seq_grad, ctx_size),
            scatter_true(
                gw_query.reshape(parts, n_q, width), sizes, places, near + across + along, jnp.bfloat16
            ),
            scatter_true(kv_terms, sizes, places, near + across[::-1] + along, jnp.bfloat16),
            scatter_true(
                gw_out.reshape(parts, n_o, width), sizes, places, near + along + across, jnp.bfloat16
            ),
            scatter_true(gs_all, sizes, places, near + across + along, jnp.float32),
            resume(ffn_chain.send([ffn_got]), ffn_chain),
        )
        grad_tok_n, _ = norm_backward(tok_f, inv_in, scale_in, own_grad + seq_part)
        grad_tokens = grad_resid + grad_tok_n
        return (
            result.reshape(seq_count, local_tok, width),
            grad_tokens.reshape(seq_count, local_tok, width),
            gs_own,
            query_grads.T,
            kv_grads[:n_k].T,
            kv_grads[n_k:].T,
            out_grads,
            ffn_grads[:n_f].T,
            ffn_grads[n_f : 2 * n_f].T,
            ffn_grads[2 * n_f :],
        )

    return on_device


def solution(mesh):
    return jax.shard_map(
        make_on_device(mesh.shape["dp"], mesh.shape["context"]),
        mesh=mesh,
        in_specs=(
            P("dp", "context", None),
            P(),
            P(("dp", "context")),
            P(None, ("dp", "context")),
            P(None, ("dp", "context")),
            P(None, ("dp", "context")),
            P(("dp", "context"), None),
            P(None, ("dp", "context")),
            P(None, ("dp", "context")),
            P(("dp", "context"), None),
            P("dp", "context", None),
        ),
        out_specs=(
            P("dp", "context", None),
            P("dp", "context", None),
            P(("dp", "context")),
            P(None, ("dp", "context")),
            P(None, ("dp", "context")),
            P(None, ("dp", "context")),
            P(("dp", "context"), None),
            P(None, ("dp", "context")),
            P(None, ("dp", "context")),
            P(("dp", "context"), None),
        ),
        check_vma=False,
    )
```
